32 devices in a mesh: shard: 8 (over z, x), blk: 4 (over y, core).
Axes of the slice: x: 2, y: 2, z: 4, core: 2. Of those that a mesh axis runs over, the one named last changes fastest.
Arguments:
- query_vectors: bfloat16 [8192, 256], P(('shard', 'blk')), may hold values from -6 to 6
- holding_devices: int32 [8192, 4], P(('shard', 'blk')), may hold values from 0 to 31, all different within a row; in each aligned block of 256 rows (0 to 255, 256 to 511, ...) at most 64 rows name the same one
- local_slot_number: int32 [8192, 4], P(('shard', 'blk')), may hold values from 0 to 4095
- valid_item_tally: int32 [8192], P(('shard', 'blk')), may hold values from 1 to 4
- score_stretch: float32 [1], replicated, may hold values from 1 to 4
- offset_term: float32 [1], replicated, may hold values from -4 to -1
- item_embedding_matrix: float32 [131072, 256], P(('shard', 'blk')), may hold values from -0.5 to 0.5
- running_grad_energy: float32 [131072, 256], P(('shard', 'blk')), may hold values from 1e-05 to 0.001
Outputs:
- table_out: float32 [131072, 256], P(('shard', 'blk'))
- new_square_sums: float32 [131072, 256], P(('shard', 'blk'))
The draws below stay inside these ranges and needn't reach their ends.
Inputs may be any that keep to these rules, and one draw needn't show every extreme that they name: `holding_devices`: the 4 owners listed for one example are distinct. Among the 256 examples of one device at most 64 ids name one owner, and this bound is reached.
All inputs are finite; a program needn't handle non-finite values.
Results may differ from the reference program's by a relative error of at most 0.014.
Values may be sent and summed in bfloat16 or wider, within the bound.
No kernel may reach another device: no remote copies, remote signals or barrier semaphores. Data moves between devices by JAX's collectives and lax.ppermute only.
A program may use at most 64 MiB of HBM per device.

```python
import math
import jax
import jax.numpy as jnp
import numpy as np
from jax import lax

D = 256
BAG = 4
EX_DEV = 256
ROWS_DEV = 4096
CAP = 64
GROUP = 1024
EXAMPLES = 8192
TABLE_ROWS = 131072
N_BLK = 4
DEVICES = 32


def place_ends(values, rng, low, high):
    dims = values.shape
    index_at = [jax.random.randint(jax.random.fold_in(rng, axis), (), 0, dims[axis]) for axis in range(len(dims))]
    values = values.at[tuple(index_at)].set(low)
    longest = dims.index(max(dims))
    index_at[longest] = (index_at[longest] + 1) % dims[longest]
    return values.at[tuple(index_at)].set(high)


def levels(key, dims, split, low, top_value):
    factor_of, own = 1.0, jax.random.fold_in(key, 6)
    for axis_at, blocks in split:
        heights = jnp.exp(jax.random.uniform(jax.random.fold_in(own, axis_at), (blocks,), jnp.float32, low / len(split), top_value / len(split)))
        factor_of = factor_of * jnp.repeat(heights, dims[axis_at] // blocks).reshape([-1 if axis == axis_at else 1 for axis in range(len(dims))])
    return factor_of


def rank_bounds(amount, slope):
    weights = [(1 << 20) // math.isqrt(grade ** slope) + 1 for grade in range(1, amount + 1)]
    scale = 1 + sum(weights) // (1 << 30)
    return np.cumsum(np.array([max(1, weight // scale) for weight in weights]))


def ranked_ids(own_key, extent, amount, slope):
    table = rank_bounds(amount, slope)
    pick = jax.random.randint(jax.random.fold_in(own_key, 1), extent, 0, int(table[amount - 1]))
    rank = jnp.searchsorted(jnp.asarray(table, jnp.int32), pick, side="right")
    return jax.random.permutation(jax.random.fold_in(own_key, 2), amount)[rank].astype(jnp.int32)


def deal_out(stream_key, own, number, rows, number_of, top, reach, lean):
    sequence = jax.random.permutation(stream_key, number_of)
    crowded, usual = shares(number_of, rows * top, reach, lean, True), shares(number_of, rows * top, reach, lean, False)
    places = jnp.arange(number_of)

    def named(tallies, turn):
        used = int((tallies > 0).sum())
        fixed = max(1, used // 4)
        shifted = fixed + (places - fixed + turn * (used - fixed)) % max(1, number_of - fixed)
        return jnp.zeros((number_of,), jnp.int32).at[sequence[jnp.where(places < fixed, places, shifted)]].set(jnp.asarray(tallies, jnp.int32))

    tallies = jnp.where(number % 4 == 0, named(crowded, number // 4), named(usual, number - number // 4 - 1))
    mixed = jax.random.permutation(jax.random.fold_in(own, 3), number_of)
    donor, receiver = mixed[0:number_of // 2 * 2:2], mixed[1:number_of // 2 * 2:2]
    room = jnp.minimum(tallies[donor] - 1, reach - tallies[receiver]) // 2
    room = jnp.where((donor == sequence[0]) | (receiver == sequence[0]) | (tallies[receiver] == 0), 0, jnp.maximum(room, 0))
    shifted = jax.random.randint(jax.random.fold_in(own, 4), (number_of // 2,), 0, 1 << 20) % (room + 1)
    tallies = tallies.at[donor].add(-shifted).at[receiver].add(shifted)
    items = jnp.searchsorted(jnp.cumsum(tallies), jnp.arange(rows * top), side="right").astype(jnp.int32)
    table = items.reshape(top, rows).T
    table = table[jax.random.permutation(jax.random.fold_in(own, 1), rows)]
    turn = jax.random.randint(jax.random.fold_in(own, 2), (rows, 1), 0, top)
    return jnp.take_along_axis(table, (jnp.arange(top)[None, :] + turn) % top, axis=1)


def shares(number_of, total, reach, lean, full):
    weights = [(1 << 20) // math.isqrt(standing ** lean) + 1 for standing in range(1, number_of + 1)]
    largest = reach if full else min(reach, max(-(-total // number_of), total * weights[0] // sum(weights)))
    least = 1 if total - largest >= number_of - 1 else 0
    counts, surplus = [largest] + [least] * (number_of - 1), total - largest - least * (number_of - 1)
    while surplus > 0:
        candidates = [i for i in range(1, number_of) if counts[i] < largest] or [i for i in range(1, number_of) if counts[i] < reach]
        mass, remaining = sum([weights[i] for i in candidates]), surplus
        for i in candidates:
            extra = min(reach - counts[i], max(1, remaining * weights[i] // mass), surplus)
            counts[i] = counts[i] + extra
            surplus = surplus - extra
    return np.array(counts)


def noise(own_key, shape, spread, most, split=(), kind=jnp.bfloat16):
    level = levels(own_key, shape, split, -0.22, 0.18) if split else 1.0
    drawn = jax.random.normal(own_key, shape, jnp.float32) * spread * level
    return jnp.minimum(jnp.maximum(drawn, -most), most).astype(kind)


def setup_inputs(seed: int = 0) -> dict:
    key_of = jax.random.split(jax.random.key(seed), 9)
    query_vectors = noise(key_of[0], (EXAMPLES, D), 1.0, 6.0, ((0, 32),))
    holding_devices_keys = jax.random.split(jax.random.fold_in(key_of[1], 1), EXAMPLES // EX_DEV)
    holding_devices_turns = jax.random.permutation(jax.random.fold_in(key_of[1], 3), EXAMPLES // EX_DEV)
    holding_devices = jax.vmap(lambda own, number: deal_out(jax.random.fold_in(key_of[1], 2), own, number, EX_DEV, DEVICES, BAG, CAP, 2))(holding_devices_keys, holding_devices_turns).reshape((EXAMPLES, BAG))
    local_slot_number = place_ends(ranked_ids(key_of[2], (EXAMPLES, BAG), ROWS_DEV, 2), jax.random.fold_in(key_of[2], 3), 0, ROWS_DEV - 1).astype(jnp.int32)
    valid_item_tally = place_ends(jax.random.randint(key_of[3], (EXAMPLES,), 1, BAG + 1), jax.random.fold_in(key_of[3], 1), 1, BAG).astype(jnp.int32)
    score_stretch = jnp.clip(jax.random.uniform(key_of[4], (1,), jnp.float32, 1.0, 4.0), 1.0, 4.0)
    offset_term = jnp.clip(jax.random.uniform(key_of[5], (1,), jnp.float32, -4.0, -1.0), -4.0, -1.0)
    item_embedding_matrix = noise(key_of[6], (TABLE_ROWS, D), 0.0625, 0.5, ((0, 32),), jnp.float32)
    running_grad_energy = jnp.clip(jnp.exp(math.log(0.001) - 4.6051703 * jax.random.uniform(key_of[7], (TABLE_ROWS, D), jnp.float32) ** levels(key_of[7], (TABLE_ROWS, D), ((0, 32),), -0.2, 0.2)), 9.999999747378752e-06, 0.001)
    return dict(query_vectors=query_vectors, holding_devices=holding_devices, local_slot_number=local_slot_number, valid_item_tally=valid_item_tally, score_stretch=score_stretch, offset_term=offset_term, item_embedding_matrix=item_embedding_matrix, running_grad_energy=running_grad_energy)


LEARN_RATE = 0.5
ADAGRAD_EPSILON = 1e-08

def reference(query_vectors, holding_devices, local_slot_number, valid_item_tally, score_stretch, offset_term, item_embedding_matrix, running_grad_energy):
    groups = EXAMPLES // GROUP
    score_multiplier = score_stretch[0]
    offset = offset_term[0]
    query_groups = query_vectors.reshape(groups, GROUP, D)
    item_ids = (holding_devices.astype(jnp.int32) * ROWS_DEV + local_slot_number.astype(jnp.int32)).reshape(groups, GROUP, BAG)
    length_groups = valid_item_tally.astype(jnp.int32).reshape(groups, GROUP)
    positions = jnp.arange(BAG, dtype=jnp.int32)
    block_starts = jnp.arange(N_BLK, dtype=jnp.int32) * EX_DEV

    def group_step(row_gradient, inputs):
        query_block, id_block, length_block = inputs
        in_bag = positions[None, :] < length_block[:, None]
        weight = jnp.where(in_bag, 1.0, 0.0).astype(jnp.float32) / length_block[:, None].astype(jnp.float32)
        fetched = item_embedding_matrix[id_block].astype(jnp.bfloat16)
        item_vecs = lax.optimization_barrier(jnp.sum(fetched.astype(jnp.float32) * weight[:, :, None], axis=1)).astype(jnp.bfloat16)
        item_blocks = item_vecs.reshape(N_BLK, EX_DEV, D)

        def block_grad(block_args):
            vec_block, first_row = block_args
            scores = score_multiplier * jnp.dot(query_block, vec_block.T, preferred_element_type=jnp.float32) + offset
            matched = jnp.arange(GROUP, dtype=jnp.int32)[:, None] == (first_row + jnp.arange(EX_DEV, dtype=jnp.int32))[None, :]
            labels = jnp.where(matched, 1.0, -1.0).astype(jnp.float32)
            coef = (labels * (jax.nn.sigmoid(labels * scores) - 1.0) * score_multiplier / GROUP).astype(jnp.bfloat16)
            return jnp.dot(coef.T, query_block, preferred_element_type=jnp.float32)
        item_grad = lax.map(block_grad, (item_blocks, block_starts)).reshape(GROUP, D)
        slot_grad = item_grad[:, None, :] * weight[:, :, None]
        row_gradient = row_gradient.at[id_block.reshape(-1)].add(slot_grad.reshape(GROUP * BAG, D))
        return (row_gradient, None)
    start_grad = jnp.zeros((TABLE_ROWS, D), jnp.float32)
    row_gradient, _ = lax.scan(group_step, start_grad, (query_groups, item_ids, length_groups))
    new_square_sums = running_grad_energy + row_gradient * row_gradient
    table_out = item_embedding_matrix - LEARN_RATE * row_gradient / (jnp.sqrt(new_square_sums) + ADAGRAD_EPSILON)
    return (table_out, new_square_sums)
```

```python
import functools

import jax
import jax.numpy as jnp
from jax import lax
from jax.experimental import pallas as pl
from jax.experimental.pallas import tpu as pltpu
from jax.sharding import PartitionSpec as P

LEARN_RATE = 0.5
ADAGRAD_EPSILON = 1e-08

BF16 = jnp.bfloat16
F32 = jnp.float32
I32 = jnp.int32
NT = (((1,), (1,)), ((), ()))
NN = (((1,), (0,)), ((), ()))


def dot(a, b, dims=NN):
    return lax.dot_general(a, b, dims, preferred_element_type=F32)


def one_hot(mask):
    return jnp.where(mask, 1.0, 0.0).astype(BF16)


def slot_matrix(ranks, capacity):
    devices, examples = ranks.shape
    place = lax.broadcasted_iota(I32, (capacity, examples), 0)
    return jnp.concatenate(
        [one_hot(ranks[o : o + 1, :] == place) for o in range(devices)], axis=0
    )


def ranks_of(owners, tally):
    bag, examples = owners.shape
    devices = tally[1]
    device = lax.broadcasted_iota(I32, (devices, examples), 0)
    named = jnp.zeros((devices, examples), I32)
    listed = jnp.zeros((devices, examples), I32)
    for k in range(bag):
        hit = jnp.where(owners[k : k + 1, :] == device, 1, 0)
        named = named + hit
        listed = listed + jnp.where(k < tally[0], hit, 0)
    earlier = one_hot(
        lax.broadcasted_iota(I32, (examples, examples), 0)
        < lax.broadcasted_iota(I32, (examples, examples), 1)
    )
    rank = dot(named.astype(F32).astype(BF16), earlier).astype(I32)
    return jnp.where(named > 0, rank, -1), jnp.where(listed > 0, rank, -1)


def route_kernel(owners_ref, rows_ref, tally_ref, requests_ref, listed_ref):
    devices, capacity = requests_ref.shape
    owners = owners_ref[...]
    rows = rows_ref[...]
    bag, examples = owners.shape
    named_rank, listed_rank = ranks_of(owners, (tally_ref[...], devices))
    listed_ref[...] = listed_rank
    slots = slot_matrix(named_rank, capacity)
    values = jnp.concatenate([rows >> 6, rows & 63, owners + 1], axis=0)
    values = jnp.concatenate([values, jnp.zeros((16 - 3 * bag, examples), I32)], axis=0)
    picked = dot(values.astype(F32).astype(BF16), slots, NT)
    owner = (lax.broadcasted_iota(I32, (1, devices * capacity), 1) // capacity + 1).astype(F32)
    found = jnp.zeros((1, devices * capacity), F32)
    for k in range(bag):
        row = picked[k : k + 1] * 64.0 + picked[bag + k : bag + k + 1] + 1.0
        found = found + jnp.where(picked[2 * bag + k : 2 * bag + k + 1] == owner, row, 0.0)
    found = found.astype(I32) - 1
    for o in range(devices):
        requests_ref[o : o + 1, :] = found[:, o * capacity : (o + 1) * capacity]


def prepare_kernel(listed_ref, tally_ref, into_ref, out_ref, share_ref, *, capacity):
    examples = listed_ref.shape[1]
    slots = slot_matrix(listed_ref[...], capacity)
    into_ref[...] = slots
    same = one_hot(
        lax.broadcasted_iota(I32, (examples, examples), 0)
        == lax.broadcasted_iota(I32, (examples, examples), 1)
    )
    out_ref[...] = dot(same, slots, NT).astype(BF16)
    share = 1.0 / tally_ref[...].astype(F32)
    share_ref[...] = jnp.broadcast_to(share, (128, examples)).T


def fetch_kernel(wanted_ref, table_ref, rows_ref, column_ref, *, step_rows):
    devices, capacity = wanted_ref.shape
    slots = devices * capacity
    width = table_ref.shape[0]
    block = pl.program_id(0)

    @pl.when(block == 0)
    def _():
        turned = wanted_ref[...].astype(F32).T.astype(I32)
        for s in range(devices):
            column_ref[s * capacity : (s + 1) * capacity, :] = jnp.broadcast_to(
                turned[:, s : s + 1], (capacity, 128)
            )
        rows_ref[...] = jnp.zeros(rows_ref.shape, BF16)

    table = table_ref[...].astype(BF16)
    lane = lax.broadcasted_iota(I32, (step_rows, 128), 1) + block * width
    for m in range(0, slots, step_rows):
        ids = column_ref[m : m + step_rows, :] - lane
        hot = jnp.concatenate([one_hot(ids == t) for t in range(0, width, 128)], axis=1)
        rows_ref[m : m + step_rows, :] += dot(hot, table).astype(BF16)


def loss_kernel(scale_ref, offset_ref, answered_ref, into_ref, out_ref, share_ref, *rest):
    queries, sent_ref = rest[:-1], rest[-1]
    examples, width = queries[0].shape
    scale = scale_ref[0]
    offset = offset_ref[0]
    grad_scale = scale / (examples * len(queries))
    share = jnp.concatenate([share_ref[...]] * (width // 128), axis=1)
    items = (dot(out_ref[...], answered_ref[...]) * share).astype(BF16)
    grad = jnp.zeros((examples, width), F32)
    for part, query_ref in enumerate(queries):
        query = query_ref[...]
        chance = jax.nn.sigmoid(scale * dot(items, query, NT) + offset)
        if part == 0:
            own = lax.broadcasted_iota(I32, (examples, examples), 0) == lax.broadcasted_iota(
                I32, (examples, examples), 1
            )
            chance = chance - jnp.where(own, 1.0, 0.0)
        grad = grad + dot((chance * grad_scale).astype(BF16), query)
    sent_ref[...] = dot(into_ref[...], (grad * share).astype(BF16)).astype(BF16)


def update_kernel(wanted_ref, incoming_ref, table_ref, energy_ref, table_out_ref, energy_out_ref, row_ref):
    devices, capacity = wanted_ref.shape
    block_rows = table_ref.shape[0]
    block = pl.program_id(0)

    @pl.when(block == 0)
    def _():
        for s in range(devices):
            row_ref[:, s * capacity : (s + 1) * capacity] = jnp.broadcast_to(
                wanted_ref[s : s + 1, :], (8, capacity)
            )

    place = lax.broadcasted_iota(I32, (block_rows, 128), 0) + block * block_rows
    hot = jnp.concatenate(
        [
            one_hot(jnp.broadcast_to(row_ref[0:1, c : c + 128], (block_rows, 128)) == place)
            for c in range(0, devices * capacity, 128)
        ],
        axis=1,
    )
    grad = dot(hot, incoming_ref[...])
    energy = energy_ref[...] + grad * grad
    energy_out_ref[...] = energy
    table_out_ref[...] = table_ref[...] - LEARN_RATE * grad / (jnp.sqrt(energy) + ADAGRAD_EPSILON)


def per_device(
    query_vectors,
    holding_devices,
    local_slot_number,
    valid_item_tally,
    score_stretch,
    offset_term,
    item_embedding_matrix,
    running_grad_energy,
):
    axes = ("shard", "blk")
    examples, bag = holding_devices.shape
    table_rows, width = item_embedding_matrix.shape
    devices = lax.axis_size(axes)
    blocks = lax.axis_size("blk")
    capacity = max(2, 2 * examples * bag // devices)
    slots = devices * capacity
    exchange = functools.partial(
        lax.all_to_all, axis_name=axes, split_axis=0, concat_axis=0, tiled=True
    )
    params = pltpu.CompilerParams(vmem_limit_bytes=40 * 1024 * 1024)
    tally = valid_item_tally.reshape(1, examples)

    requests, listed = pl.pallas_call(
        route_kernel,
        out_shape=(
            jax.ShapeDtypeStruct((devices, capacity), I32),
            jax.ShapeDtypeStruct((devices, examples), I32),
        ),
        name="route",
    )(holding_devices.T, local_slot_number.T, tally)
    wanted = exchange(requests)

    queries = [query_vectors]
    for step in range(1, blocks):
        queries.append(
            lax.ppermute(query_vectors, "blk", [(b, (b + step) % blocks) for b in range(blocks)])
        )
    into, out, share = pl.pallas_call(
        functools.partial(prepare_kernel, capacity=capacity),
        out_shape=(
            jax.ShapeDtypeStruct((slots, examples), BF16),
            jax.ShapeDtypeStruct((examples, slots), BF16),
            jax.ShapeDtypeStruct((examples, 128), F32),
        ),
        name="prepare",
    )(listed, tally)

    block = 1024
    fetched = pl.pallas_call(
        functools.partial(fetch_kernel, step_rows=256),
        grid=(table_rows // block,),
        in_specs=[
            pl.BlockSpec((devices, capacity), lambda i: (0, 0)),
            pl.BlockSpec((block, width), lambda i: (i, 0)),
        ],
        out_specs=pl.BlockSpec((slots, width), lambda i: (0, 0)),
        out_shape=jax.ShapeDtypeStruct((slots, width), BF16),
        scratch_shapes=[pltpu.VMEM((slots, 128), I32)],
        compiler_params=params,
        name="fetch",
    )(wanted, item_embedding_matrix)
    answered = exchange(fetched.reshape(devices, capacity, width)).reshape(slots, width)

    smem = pl.BlockSpec(memory_space=pltpu.SMEM)
    vmem = pl.BlockSpec(memory_space=pltpu.VMEM)
    sent = pl.pallas_call(
        loss_kernel,
        in_specs=[smem, smem] + [vmem] * (4 + blocks),
        out_shape=jax.ShapeDtypeStruct((slots, width), BF16),
        compiler_params=params,
        name="loss",
    )(score_stretch, offset_term, answered, into, out, share, *queries)
    incoming = exchange(sent.reshape(devices, capacity, width)).reshape(slots, width)

    block = 512
    rows = pl.BlockSpec((block, width), lambda i: (i, 0))
    return pl.pallas_call(
        update_kernel,
        grid=(table_rows // block,),
        in_specs=[
            pl.BlockSpec((devices, capacity), lambda i: (0, 0)),
            pl.BlockSpec((slots, width), lambda i: (0, 0)),
            rows,
            rows,
        ],
        out_specs=(rows, rows),
        out_shape=(
            jax.ShapeDtypeStruct((table_rows, width), F32),
            jax.ShapeDtypeStruct((table_rows, width), F32),
        ),
        scratch_shapes=[pltpu.VMEM((8, slots), I32)],
        compiler_params=params,
        name="update",
    )(wanted, incoming, item_embedding_matrix, running_grad_energy)


def solution(mesh):
    rows = P(("shard", "blk"), None)
    placed = (rows, rows, rows, P(("shard", "blk")), P(), P(), rows, rows)
    return jax.shard_map(
        per_device, mesh=mesh, in_specs=placed, out_specs=(rows, rows), check_vma=False
    )
```

```python
import functools

import jax
import jax.numpy as jnp
from jax import lax
from jax.experimental import pallas as pl
from jax.experimental.pallas import tpu as pltpu
from jax.sharding import PartitionSpec as P

LEARN_RATE = 0.5
ADAGRAD_EPSILON = 1e-08

BF16 = jnp.bfloat16
F32 = jnp.float32
I32 = jnp.int32
NT = (((1,), (1,)), ((), ()))
NN = (((1,), (0,)), ((), ()))


def dot(a, b, dims=NN):
    return lax.dot_general(a, b, dims, preferred_element_type=F32)


def one_hot(mask):
    return jnp.where(mask, 1.0, 0.0).astype(BF16)


def slot_matrix(ranks, capacity):
    devices, examples = ranks.shape
    place = lax.broadcasted_iota(I32, (capacity, examples), 0)
    return jnp.concatenate(
        [one_hot(ranks[o : o + 1, :] == place) for o in range(devices)], axis=0
    )


def ranks_of(owners, tally):
    bag, examples = owners.shape
    devices = tally[1]
    device = lax.broadcasted_iota(I32, (devices, examples), 0)
    named = jnp.zeros((devices, examples), I32)
    listed = jnp.zeros((devices, examples), I32)
    for k in range(bag):
        hit = jnp.where(owners[k : k + 1, :] == device, 1, 0)
        named = named + hit
        listed = listed + jnp.where(k < tally[0], hit, 0)
    earlier = one_hot(
        lax.broadcasted_iota(I32, (examples, examples), 0)
        < lax.broadcasted_iota(I32, (examples, examples), 1)
    )
    rank = dot(named.astype(F32).astype(BF16), earlier).astype(I32)
    return jnp.where(named > 0, rank, -1), jnp.where(listed > 0, rank, -1)


def route_kernel(owners_ref, rows_ref, tally_ref, requests_ref, listed_ref):
    devices, capacity = requests_ref.shape
    owners = owners_ref[...]
    rows = rows_ref[...]
    bag, examples = owners.shape
    named_rank, listed_rank = ranks_of(owners, (tally_ref[...], devices))
    listed_ref[...] = listed_rank
    slots = slot_matrix(named_rank, capacity)
    values = jnp.concatenate([rows >> 6, rows & 63, owners + 1], axis=0)
    values = jnp.concatenate([values, jnp.zeros((16 - 3 * bag, examples), I32)], axis=0)
    picked = dot(values.astype(F32).astype(BF16), slots, NT)
    owner = (lax.broadcasted_iota(I32, (1, devices * capacity), 1) // capacity + 1).astype(F32)
    found = jnp.zeros((1, devices * capacity), F32)
    for k in range(bag):
        row = picked[k : k + 1] * 64.0 + picked[bag + k : bag + k + 1] + 1.0
        found = found + jnp.where(picked[2 * bag + k : 2 * bag + k + 1] == owner, row, 0.0)
    found = found.astype(I32) - 1
    for o in range(devices):
        requests_ref[o : o + 1, :] = found[:, o * capacity : (o + 1) * capacity]


def prepare_kernel(listed_ref, tally_ref, into_ref, out_ref, share_ref, *, capacity):
    examples = listed_ref.shape[1]
    slots = slot_matrix(listed_ref[...], capacity)
    into_ref[...] = slots
    same = one_hot(
        lax.broadcasted_iota(I32, (examples, examples), 0)
        == lax.broadcasted_iota(I32, (examples, examples), 1)
    )
    out_ref[...] = dot(same, slots, NT).astype(BF16)
    share = 1.0 / tally_ref[...].astype(F32)
    share_ref[...] = jnp.broadcast_to(share, (128, examples)).T


def fetch_kernel(wanted_ref, table_ref, rows_ref, column_ref, *, step_rows, block):
    devices, capacity = wanted_ref.shape
    slots = devices * capacity
    turned = wanted_ref[...].astype(F32).T.astype(I32)
    for s in range(devices):
        column_ref[s * capacity : (s + 1) * capacity, :] = jnp.broadcast_to(
            turned[:, s : s + 1], (capacity, 128)
        )
    lane = lax.broadcasted_iota(I32, (step_rows, 128), 1)
    for b in range(table_ref.shape[0] // block):
        table = table_ref[b * block : (b + 1) * block, :].astype(BF16)
        for m in range(0, slots, step_rows):
            ids = column_ref[m : m + step_rows, :] - lane
            hot = jnp.concatenate(
                [one_hot(ids == b * block + t) for t in range(0, block, 128)], axis=1
            )
            rows = dot(hot, table).astype(BF16)
            rows_ref[m : m + step_rows, :] = rows if b == 0 else rows_ref[m : m + step_rows, :] + rows


def loss_kernel(scale_ref, offset_ref, answered_ref, into_ref, out_ref, share_ref, *rest):
    queries, (sent_ref, query_ref, arrived) = rest[:-3], rest[-3:]
    examples, width = queries[0].shape
    loads = [
        pltpu.make_async_copy(query, query_ref.at[part], arrived.at[part])
        for part, query in enumerate(queries)
    ]
    for load in loads:
        load.start()
    scale = scale_ref[0]
    offset = offset_ref[0]
    grad_scale = scale / (examples * len(queries))
    share = jnp.concatenate([share_ref[...]] * (width // 128), axis=1)
    items = (dot(out_ref[...], answered_ref[...]) * share).astype(BF16)
    grad = jnp.zeros((examples, width), F32)
    for part, load in enumerate(loads):
        load.wait()
        query = query_ref[part]
        chance = jax.nn.sigmoid(scale * dot(items, query, NT) + offset)
        if part == 0:
            own = lax.broadcasted_iota(I32, (examples, examples), 0) == lax.broadcasted_iota(
                I32, (examples, examples), 1
            )
            chance = chance - jnp.where(own, 1.0, 0.0)
        grad = grad + dot((chance * grad_scale).astype(BF16), query)
    sent_ref[...] = dot(into_ref[...], (grad * share).astype(BF16)).astype(BF16)


def update_kernel(
    wanted_ref, incoming_ref, table_ref, energy_ref, table_out_ref, energy_out_ref,
    row_ref, table_buf, energy_buf, table_sem, energy_sem,
):
    devices, capacity = wanted_ref.shape
    slots, _ = incoming_ref.shape
    block = table_buf.shape[1]
    blocks = table_ref.shape[0] // block
    for s in range(devices):
        row_ref[:, s * capacity : (s + 1) * capacity] = jnp.broadcast_to(
            wanted_ref[s : s + 1, :], (8, capacity)
        )
    place = lax.broadcasted_iota(I32, (block, 128), 0)

    def stores(b, half):
        at = pl.ds(pl.multiple_of(b * block, block), block)
        return (
            pltpu.make_async_copy(table_buf.at[half], table_out_ref.at[at, :], table_sem.at[half]),
            pltpu.make_async_copy(energy_buf.at[half], energy_out_ref.at[at, :], energy_sem.at[half]),
        )

    def step(b, half):
        at = pl.ds(pl.multiple_of(b * block, block), block)
        here = place + b * block
        hot = jnp.concatenate(
            [
                one_hot(jnp.broadcast_to(row_ref[0:1, c : c + 128], (block, 128)) == here)
                for c in range(0, slots, 128)
            ],
            axis=1,
        )
        grad = dot(hot, incoming_ref[...])
        energy = energy_ref[at, :] + grad * grad
        energy_buf[half] = energy
        table_buf[half] = table_ref[at, :] - LEARN_RATE * grad / (jnp.sqrt(energy) + ADAGRAD_EPSILON)
        for store in stores(b, half):
            store.start()

    for b in range(blocks):
        half = b % 2
        if b >= 2:
            for store in stores(b - 2, half):
                store.wait()
        step(b, half)
    for b in (blocks - 2, blocks - 1):
        for store in stores(b, b % 2):
            store.wait()


def per_device(
    query_vectors,
    holding_devices,
    local_slot_number,
    valid_item_tally,
    score_stretch,
    offset_term,
    item_embedding_matrix,
    running_grad_energy,
):
    axes = ("shard", "blk")
    examples, bag = holding_devices.shape
    table_rows, width = item_embedding_matrix.shape
    devices = lax.axis_size(axes)
    blocks = lax.axis_size("blk")
    capacity = max(2, 2 * examples * bag // devices)
    slots = devices * capacity
    exchange = functools.partial(
        lax.all_to_all, axis_name=axes, split_axis=0, concat_axis=0, tiled=True
    )
    smem = pl.BlockSpec(memory_space=pltpu.SMEM)
    vmem = pl.BlockSpec(memory_space=pltpu.VMEM)
    hbm = pl.BlockSpec(memory_space=pltpu.HBM)

    def in_hbm(array):
        return pltpu.with_memory_space_constraint(array, pltpu.HBM)

    def limit(mib):
        return pltpu.CompilerParams(vmem_limit_bytes=mib * 1024 * 1024)

    def cost(gflops):
        return pl.CostEstimate(flops=gflops * 10**9, transcendentals=0, bytes_accessed=10**6)

    tally = valid_item_tally.reshape(1, examples)

    requests, listed = pl.pallas_call(
        route_kernel,
        out_shape=(
            jax.ShapeDtypeStruct((devices, capacity), I32),
            jax.ShapeDtypeStruct((devices, examples), I32),
        ),
        compiler_params=limit(4),
        cost_estimate=cost(10),
        name="route",
    )(in_hbm(holding_devices.T), in_hbm(local_slot_number.T), in_hbm(tally))
    wanted = exchange(requests)

    queries = [query_vectors]
    for step in range(1, blocks):
        queries.append(
            lax.ppermute(query_vectors, "blk", [(b, (b + step) % blocks) for b in range(blocks)])
        )
    into, out, share = pl.pallas_call(
        functools.partial(prepare_kernel, capacity=capacity),
        out_shape=(
            jax.ShapeDtypeStruct((slots, examples), BF16),
            jax.ShapeDtypeStruct((examples, slots), BF16),
            jax.ShapeDtypeStruct((examples, 128), F32),
        ),
        compiler_params=limit(8),
        name="prepare",
    )(listed, in_hbm(tally))

    fetched = pl.pallas_call(
        functools.partial(fetch_kernel, step_rows=256, block=1024),
        in_specs=[vmem, vmem],
        out_shape=jax.ShapeDtypeStruct((slots, width), BF16),
        scratch_shapes=[pltpu.VMEM((slots, 128), I32)],
        compiler_params=limit(12),
        name="fetch",
    )(wanted, item_embedding_matrix)
    answered = exchange(fetched.reshape(devices, capacity, width)).reshape(slots, width)

    sent = pl.pallas_call(
        loss_kernel,
        in_specs=[smem, smem] + [vmem] * 4 + [hbm] * blocks,
        out_shape=jax.ShapeDtypeStruct((slots, width), BF16),
        scratch_shapes=[
            pltpu.VMEM((blocks, examples, width), BF16),
            pltpu.SemaphoreType.DMA((blocks,)),
        ],
        compiler_params=limit(12),
        cost_estimate=cost(30),
        name="loss",
    )(score_stretch, offset_term, answered, into, out, share, *map(in_hbm, queries))
    incoming = exchange(sent.reshape(devices, capacity, width)).reshape(slots, width)

    block = 512
    return pl.pallas_call(
        update_kernel,
        in_specs=[vmem] * 4,
        out_specs=(hbm, hbm),
        out_shape=(
            jax.ShapeDtypeStruct((table_rows, width), F32),
            jax.ShapeDtypeStruct((table_rows, width), F32),
        ),
        scratch_shapes=[
            pltpu.VMEM((8, slots), I32),
            pltpu.VMEM((2, block, width), F32),
            pltpu.VMEM((2, block, width), F32),
            pltpu.SemaphoreType.DMA((2,)),
            pltpu.SemaphoreType.DMA((2,)),
        ],
        compiler_params=limit(16),
        name="update",
    )(wanted, incoming, item_embedding_matrix, running_grad_energy)


def solution(mesh):
    rows = P(("shard", "blk"), None)
    placed = (rows, rows, rows, P(("shard", "blk")), P(), P(), rows, rows)
    return jax.shard_map(
        per_device, mesh=mesh, in_specs=placed, out_specs=(rows, rows), check_vma=False
    )
```

```python
import functools

import jax
import jax.numpy as jnp
from jax import lax
from jax.experimental import pallas as pl
from jax.experimental.pallas import tpu as pltpu
from jax.sharding import PartitionSpec as P

LEARN_RATE = 0.5
ADAGRAD_EPSILON = 1e-08

BF16 = jnp.bfloat16
F32 = jnp.float32
I32 = jnp.int32
NT = (((1,), (1,)), ((), ()))
NN = (((1,), (0,)), ((), ()))


def dot(a, b, dims=NN):
    return lax.dot_general(a, b, dims, preferred_element_type=F32)


def one_hot(mask):
    return jnp.where(mask, 1.0, 0.0).astype(BF16)


def slot_matrix(ranks, capacity):
    devices, examples = ranks.shape
    place = lax.broadcasted_iota(I32, (capacity, examples), 0)
    return jnp.concatenate(
        [one_hot(ranks[o : o + 1, :] == place) for o in range(devices)], axis=0
    )


def ranks_of(owners, tally):
    bag, examples = owners.shape
    devices = tally[1]
    device = lax.broadcasted_iota(I32, (devices, examples), 0)
    named = jnp.zeros((devices, examples), I32)
    listed = jnp.zeros((devices, examples), I32)
    for k in range(bag):
        hit = jnp.where(owners[k : k + 1, :] == device, 1, 0)
        named = named + hit
        listed = listed + jnp.where(k < tally[0], hit, 0)
    earlier = one_hot(
        lax.broadcasted_iota(I32, (examples, examples), 0)
        < lax.broadcasted_iota(I32, (examples, examples), 1)
    )
    rank = dot(named.astype(F32).astype(BF16), earlier).astype(I32)
    return jnp.where(named > 0, rank, -1), jnp.where(listed > 0, rank, -1)


def route_kernel(owners_ref, rows_ref, tally_ref, requests_ref, listed_ref):
    devices, capacity = requests_ref.shape
    owners = owners_ref[...]
    rows = rows_ref[...]
    bag, examples = owners.shape
    named_rank, listed_rank = ranks_of(owners, (tally_ref[...], devices))
    listed_ref[...] = listed_rank
    slots = slot_matrix(named_rank, capacity)
    values = jnp.concatenate([rows >> 6, rows & 63, owners + 1], axis=0)
    values = jnp.concatenate([values, jnp.zeros((16 - 3 * bag, examples), I32)], axis=0)
    picked = dot(values.astype(F32).astype(BF16), slots, NT)
    owner = (lax.broadcasted_iota(I32, (1, devices * capacity), 1) // capacity + 1).astype(F32)
    found = jnp.zeros((1, devices * capacity), F32)
    for k in range(bag):
        row = picked[k : k + 1] * 64.0 + picked[bag + k : bag + k + 1] + 1.0
        found = found + jnp.where(picked[2 * bag + k : 2 * bag + k + 1] == owner, row, 0.0)
    found = found.astype(I32) - 1
    for o in range(devices):
        requests_ref[o : o + 1, :] = found[:, o * capacity : (o + 1) * capacity]


def prepare_kernel(listed_ref, tally_ref, out_ref, share_ref, *, capacity):
    examples = listed_ref.shape[1]
    slots = slot_matrix(listed_ref[...], capacity)
    same = one_hot(
        lax.broadcasted_iota(I32, (examples, examples), 0)
        == lax.broadcasted_iota(I32, (examples, examples), 1)
    )
    out_ref[...] = dot(same, slots, NT).astype(BF16)
    share = 1.0 / tally_ref[...].astype(F32)
    share_ref[...] = jnp.broadcast_to(share, (128, examples)).T


def fetch_kernel(wanted_ref, table_ref, rows_ref, column_ref, *, step_rows, block):
    devices, capacity = wanted_ref.shape
    slots = devices * capacity
    turned = wanted_ref[...].astype(F32).T.astype(I32)
    for s in range(devices):
        column_ref[s * capacity : (s + 1) * capacity, :] = jnp.broadcast_to(
            turned[:, s : s + 1], (capacity, 128)
        )
    lane = lax.broadcasted_iota(I32, (step_rows, 128), 1)
    for b in range(table_ref.shape[0] // block):
        table = table_ref[b * block : (b + 1) * block, :].astype(BF16)
        for m in range(0, slots, step_rows):
            ids = column_ref[m : m + step_rows, :] - lane
            hot = jnp.concatenate(
                [one_hot(ids == b * block + t) for t in range(0, block, 128)], axis=1
            )
            rows = dot(hot, table).astype(BF16)
            rows_ref[m : m + step_rows, :] = rows if b == 0 else rows_ref[m : m + step_rows, :] + rows


def loss_kernel(scale_ref, offset_ref, answered_ref, listed_ref, out_ref, share_ref, *rest, capacity):
    queries, sent_ref = rest[:-1], rest[-1]
    examples, width = queries[0].shape
    scale = scale_ref[0]
    offset = offset_ref[0]
    grad_scale = scale / (examples * len(queries))
    share = jnp.concatenate([share_ref[...]] * (width // 128), axis=1)
    items = (dot(out_ref[...], answered_ref[...]) * share).astype(BF16)
    grad = jnp.zeros((examples, width), F32)
    for part, query_ref in enumerate(queries):
        query = query_ref[...]
        chance = jax.nn.sigmoid(scale * dot(items, query, NT) + offset)
        if part == 0:
            own = lax.broadcasted_iota(I32, (examples, examples), 0) == lax.broadcasted_iota(
                I32, (examples, examples), 1
            )
            chance = chance - jnp.where(own, 1.0, 0.0)
        grad = grad + dot((chance * grad_scale).astype(BF16), query)
    slots = slot_matrix(listed_ref[...], capacity)
    sent_ref[...] = dot(slots, (grad * share).astype(BF16)).astype(BF16)


def update_kernel(
    wanted_ref, incoming_ref, table_ref, energy_ref, table_out_ref, energy_out_ref,
    row_ref, table_buf, energy_buf, table_sem, energy_sem,
):
    devices, capacity = wanted_ref.shape
    slots, _ = incoming_ref.shape
    block = table_buf.shape[1]
    blocks = table_ref.shape[0] // block
    for s in range(devices):
        row_ref[:, s * capacity : (s + 1) * capacity] = jnp.broadcast_to(
            wanted_ref[s : s + 1, :], (8, capacity)
        )
    place = lax.broadcasted_iota(I32, (block, 128), 0)

    def stores(b, half):
        at = pl.ds(pl.multiple_of(b * block, block), block)
        return (
            pltpu.make_async_copy(table_buf.at[half], table_out_ref.at[at, :], table_sem.at[half]),
            pltpu.make_async_copy(energy_buf.at[half], energy_out_ref.at[at, :], energy_sem.at[half]),
        )

    def step(b, half):
        at = pl.ds(pl.multiple_of(b * block, block), block)
        here = place + b * block
        hot = jnp.concatenate(
            [
                one_hot(jnp.broadcast_to(row_ref[0:1, c : c + 128], (block, 128)) == here)
                for c in range(0, slots, 128)
            ],
            axis=1,
        )
        grad = dot(hot, incoming_ref[...])
        energy = energy_ref[at, :] + grad * grad
        energy_buf[half] = energy
        table_buf[half] = table_ref[at, :] - LEARN_RATE * grad / (jnp.sqrt(energy) + ADAGRAD_EPSILON)
        for store in stores(b, half):
            store.start()

    buffers = table_buf.shape[0]

    def turn(b, carry):
        half = lax.rem(b, buffers)

        @pl.when(b >= buffers)
        def _():
            for store in stores(b - buffers, half):
                store.wait()

        step(b, half)
        return carry

    lax.fori_loop(0, blocks, turn, 0)
    for b in range(blocks - buffers, blocks):
        for store in stores(b, b % buffers):
            store.wait()


def per_device(
    query_vectors,
    holding_devices,
    local_slot_number,
    valid_item_tally,
    score_stretch,
    offset_term,
    item_embedding_matrix,
    running_grad_energy,
):
    axes = ("shard", "blk")
    examples, bag = holding_devices.shape
    table_rows, width = item_embedding_matrix.shape
    devices = lax.axis_size(axes)
    blocks = lax.axis_size("blk")
    capacity = max(2, 2 * examples * bag // devices)
    slots = devices * capacity
    exchange = functools.partial(
        lax.all_to_all, axis_name=axes, split_axis=0, concat_axis=0, tiled=True
    )
    smem = pl.BlockSpec(memory_space=pltpu.SMEM)
    vmem = pl.BlockSpec(memory_space=pltpu.VMEM)
    hbm = pl.BlockSpec(memory_space=pltpu.HBM)

    def in_hbm(array):
        return pltpu.with_memory_space_constraint(array, pltpu.HBM)

    def limit(mib):
        return pltpu.CompilerParams(vmem_limit_bytes=mib * 1024 * 1024)

    def cost(gflops):
        return pl.CostEstimate(flops=gflops * 10**9, transcendentals=0, bytes_accessed=10**6)

    tally = valid_item_tally.reshape(1, examples)

    requests, listed = pl.pallas_call(
        route_kernel,
        out_shape=(
            jax.ShapeDtypeStruct((devices, capacity), I32),
            jax.ShapeDtypeStruct((devices, examples), I32),
        ),
        compiler_params=limit(4),
        cost_estimate=cost(10),
        name="route",
    )(in_hbm(holding_devices.T), in_hbm(local_slot_number.T), in_hbm(tally))
    wanted = exchange(requests)

    queries = [query_vectors]
    for step in range(1, blocks):
        queries.append(
            lax.ppermute(query_vectors, "blk", [(b, (b + step) % blocks) for b in range(blocks)])
        )
    out, share = pl.pallas_call(
        functools.partial(prepare_kernel, capacity=capacity),
        out_shape=(
            jax.ShapeDtypeStruct((examples, slots), BF16),
            jax.ShapeDtypeStruct((examples, 128), F32),
        ),
        compiler_params=limit(8),
        name="prepare",
    )(listed, in_hbm(tally))

    fetched = pl.pallas_call(
        functools.partial(fetch_kernel, step_rows=256, block=1024),
        in_specs=[vmem, vmem],
        out_shape=jax.ShapeDtypeStruct((slots, width), BF16),
        scratch_shapes=[pltpu.VMEM((slots, 128), I32)],
        compiler_params=limit(12),
        name="fetch",
    )(wanted, item_embedding_matrix)
    answered = exchange(fetched.reshape(devices, capacity, width)).reshape(slots, width)

    sent = pl.pallas_call(
        functools.partial(loss_kernel, capacity=capacity),
        in_specs=[smem, smem] + [vmem] * (4 + blocks),
        out_shape=jax.ShapeDtypeStruct((slots, width), BF16),
        compiler_params=limit(12),
        cost_estimate=cost(30),
        name="loss",
    )(score_stretch, offset_term, answered, listed, out, share, *queries)
    incoming = exchange(sent.reshape(devices, capacity, width)).reshape(slots, width)

    block = 512
    return pl.pallas_call(
        update_kernel,
        in_specs=[vmem] * 4,
        out_specs=(hbm, hbm),
        out_shape=(
            jax.ShapeDtypeStruct((table_rows, width), F32),
            jax.ShapeDtypeStruct((table_rows, width), F32),
        ),
        scratch_shapes=[
            pltpu.VMEM((8, slots), I32),
            pltpu.VMEM((4, block, width), F32),
            pltpu.VMEM((4, block, width), F32),
            pltpu.SemaphoreType.DMA((4,)),
            pltpu.SemaphoreType.DMA((4,)),
        ],
        compiler_params=limit(16),
        name="update",
    )(wanted, incoming, item_embedding_matrix, running_grad_energy)


def solution(mesh):
    rows = P(("shard", "blk"), None)
    placed = (rows, rows, rows, P(("shard", "blk")), P(), P(), rows, rows)
    return jax.shard_map(
        per_device, mesh=mesh, in_specs=placed, out_specs=(rows, rows), check_vma=False
    )
```

```python
import functools

import jax
import jax.numpy as jnp
from jax import lax
from jax.experimental import pallas as pl
from jax.experimental.pallas import tpu as pltpu
from jax.sharding import PartitionSpec as P

LEARN_RATE = 0.5
ADAGRAD_EPSILON = 1e-08

BF16 = jnp.bfloat16
F32 = jnp.float32
I32 = jnp.int32
NT = (((1,), (1,)), ((), ()))
NN = (((1,), (0,)), ((), ()))


def dot(a, b, dims=NN):
    return lax.dot_general(a, b, dims, preferred_element_type=F32)


def one_hot(mask):
    return jnp.where(mask, 1.0, 0.0).astype(BF16)


def slot_matrix(ranks, capacity):
    devices, examples = ranks.shape
    place = lax.broadcasted_iota(I32, (capacity, examples), 0)
    return jnp.concatenate(
        [one_hot(ranks[o : o + 1, :] == place) for o in range(devices)], axis=0
    )


def ranks_of(owners, tally):
    bag, examples = owners.shape
    devices = tally[1]
    device = lax.broadcasted_iota(I32, (devices, examples), 0)
    named = jnp.zeros((devices, examples), I32)
    listed = jnp.zeros((devices, examples), I32)
    for k in range(bag):
        hit = jnp.where(owners[k : k + 1, :] == device, 1, 0)
        named = named + hit
        listed = listed + jnp.where(k < tally[0], hit, 0)
    earlier = one_hot(
        lax.broadcasted_iota(I32, (examples, examples), 0)
        < lax.broadcasted_iota(I32, (examples, examples), 1)
    )
    rank = dot(named.astype(F32).astype(BF16), earlier).astype(I32)
    return jnp.where(named > 0, rank, -1), jnp.where(listed > 0, rank, -1)


def route_kernel(owners_ref, rows_ref, tally_ref, requests_ref, listed_ref):
    devices, capacity = requests_ref.shape
    owners = owners_ref[...]
    rows = rows_ref[...]
    bag, examples = owners.shape
    named_rank, listed_rank = ranks_of(owners, (tally_ref[...], devices))
    listed_ref[...] = listed_rank
    slots = slot_matrix(named_rank, capacity)
    values = jnp.concatenate([rows >> 6, rows & 63, owners + 1], axis=0)
    values = jnp.concatenate([values, jnp.zeros((16 - 3 * bag, examples), I32)], axis=0)
    picked = dot(values.astype(F32).astype(BF16), slots, NT)
    owner = (lax.broadcasted_iota(I32, (1, devices * capacity), 1) // capacity + 1).astype(F32)
    found = jnp.zeros((1, devices * capacity), F32)
    for k in range(bag):
        row = picked[k : k + 1] * 64.0 + picked[bag + k : bag + k + 1] + 1.0
        found = found + jnp.where(picked[2 * bag + k : 2 * bag + k + 1] == owner, row, 0.0)
    found = found.astype(I32) - 1
    for o in range(devices):
        requests_ref[o : o + 1, :] = found[:, o * capacity : (o + 1) * capacity]


def prepare_kernel(listed_ref, tally_ref, out_ref, share_ref, *, capacity):
    examples = listed_ref.shape[1]
    slots = slot_matrix(listed_ref[...], capacity)
    same = one_hot(
        lax.broadcasted_iota(I32, (examples, examples), 0)
        == lax.broadcasted_iota(I32, (examples, examples), 1)
    )
    out_ref[...] = dot(same, slots, NT).astype(BF16)
    share = 1.0 / tally_ref[...].astype(F32)
    share_ref[...] = jnp.broadcast_to(share, (128, examples)).T


def fetch_kernel(wanted_ref, table_ref, rows_ref, column_ref, *, step_rows, block):
    devices, capacity = wanted_ref.shape
    slots = devices * capacity
    turned = wanted_ref[...].astype(F32).T.astype(I32)
    for s in range(devices):
        column_ref[s * capacity : (s + 1) * capacity, :] = jnp.broadcast_to(
            turned[:, s : s + 1], (capacity, 128)
        )
    lane = lax.broadcasted_iota(I32, (step_rows, 128), 1)
    for b in range(table_ref.shape[0] // block):
        table = table_ref[b * block : (b + 1) * block, :].astype(BF16)
        for m in range(0, slots, step_rows):
            ids = column_ref[m : m + step_rows, :] - lane
            hot = jnp.concatenate(
                [one_hot(ids == b * block + t) for t in range(0, block, 128)], axis=1
            )
            rows = dot(hot, table).astype(BF16)
            rows_ref[m : m + step_rows, :] = rows if b == 0 else rows_ref[m : m + step_rows, :] + rows


def loss_kernel(scale_ref, offset_ref, answered_ref, listed_ref, out_ref, share_ref, *rest, capacity):
    queries, sent_ref = rest[:-1], rest[-1]
    examples, width = queries[0].shape
    scale = scale_ref[0]
    offset = offset_ref[0]
    grad_scale = scale / (examples * len(queries))
    share = jnp.concatenate([share_ref[...]] * (width // 128), axis=1)
    items = (dot(out_ref[...], answered_ref[...]) * share).astype(BF16)
    grad = jnp.zeros((examples, width), F32)
    for part, query_ref in enumerate(queries):
        query = query_ref[...]
        chance = jax.nn.sigmoid(scale * dot(items, query, NT) + offset)
        if part == 0:
            own = lax.broadcasted_iota(I32, (examples, examples), 0) == lax.broadcasted_iota(
                I32, (examples, examples), 1
            )
            chance = chance - jnp.where(own, 1.0, 0.0)
        grad = grad + dot((chance * grad_scale).astype(BF16), query)
    slots = slot_matrix(listed_ref[...], capacity)
    sent_ref[...] = dot(slots, (grad * share).astype(BF16)).astype(BF16)


def update_kernel(
    wanted_ref, incoming_ref, table_ref, energy_ref, table_out_ref, energy_out_ref,
    row_ref, table_buf, energy_buf, sent, *, chunk, depth, piece,
):
    devices, capacity = wanted_ref.shape
    slots, _ = incoming_ref.shape
    rows = table_ref.shape[0]
    for s in range(devices):
        row_ref[:, s * capacity : (s + 1) * capacity] = jnp.broadcast_to(
            wanted_ref[s : s + 1, :], (8, capacity)
        )

    def stores(at):
        return (
            pltpu.make_async_copy(table_buf.at[at, :], table_out_ref.at[at, :], sent.at[0]),
            pltpu.make_async_copy(energy_buf.at[at, :], energy_out_ref.at[at, :], sent.at[1]),
        )

    def row_grad(base):
        here = lax.broadcasted_iota(I32, (chunk, 128), 0) + base
        total = None
        for k in range(0, slots, depth):
            hot = jnp.concatenate(
                [
                    one_hot(jnp.broadcast_to(row_ref[0:1, c : c + 128], (chunk, 128)) == here)
                    for c in range(k, k + depth, 128)
                ],
                axis=1,
            )
            part = dot(hot, incoming_ref[k : k + depth, :])
            total = part if total is None else total + part
        return total

    def adagrad(base, grad):
        at = pl.ds(pl.multiple_of(base, chunk), chunk)
        energy = energy_ref[at, :] + grad * grad
        energy_buf[at, :] = energy
        table_buf[at, :] = table_ref[at, :] - LEARN_RATE * grad / (jnp.sqrt(energy) + ADAGRAD_EPSILON)

    def sweep(i, carry):
        first = i * rows
        grad = row_grad(first)
        for q in range(chunk, rows + chunk, chunk):
            after = row_grad(first + q) if q < rows else None
            adagrad(first + q - chunk, grad)
            grad = after
            if q % piece == 0:
                for store in stores(pl.ds(pl.multiple_of(first + q - piece, piece), piece)):
                    store.start()
        return carry

    lax.fori_loop(0, 1, sweep, 0)
    for store in stores(pl.ds(0, rows)):
        store.wait()


def per_device(
    query_vectors,
    holding_devices,
    local_slot_number,
    valid_item_tally,
    score_stretch,
    offset_term,
    item_embedding_matrix,
    running_grad_energy,
):
    axes = ("shard", "blk")
    examples, bag = holding_devices.shape
    table_rows, width = item_embedding_matrix.shape
    devices = lax.axis_size(axes)
    blocks = lax.axis_size("blk")
    capacity = max(2, 2 * examples * bag // devices)
    slots = devices * capacity
    exchange = functools.partial(
        lax.all_to_all, axis_name=axes, split_axis=0, concat_axis=0, tiled=True
    )
    smem = pl.BlockSpec(memory_space=pltpu.SMEM)
    vmem = pl.BlockSpec(memory_space=pltpu.VMEM)
    hbm = pl.BlockSpec(memory_space=pltpu.HBM)

    def in_hbm(array):
        return pltpu.with_memory_space_constraint(array, pltpu.HBM)

    def limit(mib):
        return pltpu.CompilerParams(vmem_limit_bytes=mib * 1024 * 1024)

    def cost(gflops):
        return pl.CostEstimate(flops=gflops * 10**9, transcendentals=0, bytes_accessed=10**6)

    tally = valid_item_tally.reshape(1, examples)

    requests, listed = pl.pallas_call(
        route_kernel,
        out_shape=(
            jax.ShapeDtypeStruct((devices, capacity), I32),
            jax.ShapeDtypeStruct((devices, examples), I32),
        ),
        compiler_params=limit(4),
        cost_estimate=cost(10),
        name="route",
    )(in_hbm(holding_devices.T), in_hbm(local_slot_number.T), in_hbm(tally))
    wanted = exchange(requests)

    queries = [query_vectors]
    for step in range(1, blocks):
        queries.append(
            lax.ppermute(query_vectors, "blk", [(b, (b + step) % blocks) for b in range(blocks)])
        )
    out, share = pl.pallas_call(
        functools.partial(prepare_kernel, capacity=capacity),
        out_shape=(
            jax.ShapeDtypeStruct((examples, slots), BF16),
            jax.ShapeDtypeStruct((examples, 128), F32),
        ),
        compiler_params=limit(8),
        name="prepare",
    )(listed, in_hbm(tally))

    fetched = pl.pallas_call(
        functools.partial(fetch_kernel, step_rows=256, block=1024),
        in_specs=[vmem, vmem],
        out_shape=jax.ShapeDtypeStruct((slots, width), BF16),
        scratch_shapes=[pltpu.VMEM((slots, 128), I32)],
        compiler_params=limit(12),
        name="fetch",
    )(wanted, item_embedding_matrix)
    answered = exchange(fetched.reshape(devices, capacity, width)).reshape(slots, width)

    sent = pl.pallas_call(
        functools.partial(loss_kernel, capacity=capacity),
        in_specs=[smem, smem] + [vmem] * (4 + blocks),
        out_shape=jax.ShapeDtypeStruct((slots, width), BF16),
        compiler_params=limit(12),
        cost_estimate=cost(30),
        name="loss",
    )(score_stretch, offset_term, answered, listed, out, share, *queries)
    incoming = exchange(sent.reshape(devices, capacity, width)).reshape(slots, width)

    return pl.pallas_call(
        functools.partial(update_kernel, chunk=256, depth=1024, piece=512),
        in_specs=[vmem] * 4,
        out_specs=(hbm, hbm),
        out_shape=(
            jax.ShapeDtypeStruct((table_rows, width), F32),
            jax.ShapeDtypeStruct((table_rows, width), F32),
        ),
        scratch_shapes=[
            pltpu.VMEM((8, slots), I32),
            pltpu.VMEM((table_rows, width), F32),
            pltpu.VMEM((table_rows, width), F32),
            pltpu.SemaphoreType.DMA((2,)),
        ],
        compiler_params=limit(24),
        name="update",
    )(wanted, incoming, item_embedding_matrix, running_grad_energy)


def solution(mesh):
    rows = P(("shard", "blk"), None)
    placed = (rows, rows, rows, P(("shard", "blk")), P(), P(), rows, rows)
    return jax.shard_map(
        per_device, mesh=mesh, in_specs=placed, out_specs=(rows, rows), check_vma=False
    )
```

```python
import functools

import jax
import jax.numpy as jnp
from jax import lax
from jax.experimental import pallas as pl
from jax.experimental.pallas import tpu as pltpu
from jax.sharding import PartitionSpec as P

LEARN_RATE = 0.5
ADAGRAD_EPSILON = 1e-08

BF16 = jnp.bfloat16
F32 = jnp.float32
I32 = jnp.int32
NT = (((1,), (1,)), ((), ()))
NN = (((1,), (0,)), ((), ()))


def dot(a, b, dims=NN):
    return lax.dot_general(a, b, dims, preferred_element_type=F32)


def one_hot(mask):
    return jnp.where(mask, 1.0, 0.0).astype(BF16)


def slot_matrix(ranks, capacity):
    devices, examples = ranks.shape
    place = lax.broadcasted_iota(I32, (capacity, examples), 0)
    return jnp.concatenate(
        [one_hot(ranks[o : o + 1, :] == place) for o in range(devices)], axis=0
    )


def ranks_of(owners, tally):
    bag, examples = owners.shape
    devices = tally[1]
    device = lax.broadcasted_iota(I32, (devices, examples), 0)
    named = jnp.zeros((devices, examples), I32)
    listed = jnp.zeros((devices, examples), I32)
    for k in range(bag):
        hit = jnp.where(owners[k : k + 1, :] == device, 1, 0)
        named = named + hit
        listed = listed + jnp.where(k < tally[0], hit, 0)
    earlier = one_hot(
        lax.broadcasted_iota(I32, (examples, examples), 0)
        < lax.broadcasted_iota(I32, (examples, examples), 1)
    )
    rank = dot(named.astype(F32).astype(BF16), earlier).astype(I32)
    return jnp.where(named > 0, rank, -1), jnp.where(listed > 0, rank, -1)


def route_kernel(owners_ref, rows_ref, tally_ref, requests_ref, listed_ref):
    devices, capacity = requests_ref.shape
    owners = owners_ref[...]
    rows = rows_ref[...]
    bag, examples = owners.shape
    named_rank, listed_rank = ranks_of(owners, (tally_ref[...], devices))
    listed_ref[...] = listed_rank
    slots = slot_matrix(named_rank, capacity)
    values = jnp.concatenate([rows >> 6, rows & 63, owners + 1], axis=0)
    values = jnp.concatenate([values, jnp.zeros((16 - 3 * bag, examples), I32)], axis=0)
    picked = dot(values.astype(F32).astype(BF16), slots, NT)
    owner = (lax.broadcasted_iota(I32, (1, devices * capacity), 1) // capacity + 1).astype(F32)
    found = jnp.zeros((1, devices * capacity), F32)
    for k in range(bag):
        row = picked[k : k + 1] * 64.0 + picked[bag + k : bag + k + 1] + 1.0
        found = found + jnp.where(picked[2 * bag + k : 2 * bag + k + 1] == owner, row, 0.0)
    found = found.astype(I32) - 1
    for o in range(devices):
        requests_ref[o : o + 1, :] = found[:, o * capacity : (o + 1) * capacity]


def prepare_kernel(listed_ref, tally_ref, out_ref, share_ref, *, capacity):
    examples = listed_ref.shape[1]
    slots = slot_matrix(listed_ref[...], capacity)
    same = one_hot(
        lax.broadcasted_iota(I32, (examples, examples), 0)
        == lax.broadcasted_iota(I32, (examples, examples), 1)
    )
    out_ref[...] = dot(same, slots, NT).astype(BF16)
    share = 1.0 / tally_ref[...].astype(F32)
    share_ref[...] = jnp.broadcast_to(share, (128, examples)).T


def fetch_kernel(wanted_ref, table_ref, rows_ref, column_ref, *, step_rows, block):
    devices, capacity = wanted_ref.shape
    slots = devices * capacity
    turned = wanted_ref[...].astype(F32).T.astype(I32)
    for s in range(devices):
        column_ref[s * capacity : (s + 1) * capacity, :] = jnp.broadcast_to(
            turned[:, s : s + 1], (capacity, 128)
        )
    lane = lax.broadcasted_iota(I32, (step_rows, 128), 1)
    for b in range(table_ref.shape[0] // block):
        table = table_ref[b * block : (b + 1) * block, :].astype(BF16)
        for m in range(0, slots, step_rows):
            ids = column_ref[m : m + step_rows, :] - lane
            hot = jnp.concatenate(
                [one_hot(ids == b * block + t) for t in range(0, block, 128)], axis=1
            )
            rows = dot(hot, table).astype(BF16)
            rows_ref[m : m + step_rows, :] = rows if b == 0 else rows_ref[m : m + step_rows, :] + rows


def loss_kernel(scale_ref, offset_ref, answered_ref, listed_ref, out_ref, share_ref, *rest, capacity):
    queries, sent_ref = rest[:-1], rest[-1]
    examples, width = queries[0].shape
    scale = scale_ref[0]
    offset = offset_ref[0]
    grad_scale = scale / (examples * len(queries))
    share = jnp.concatenate([share_ref[...]] * (width // 128), axis=1)
    items = (dot(out_ref[...], answered_ref[...]) * share).astype(BF16)
    grad = jnp.zeros((examples, width), F32)
    for part, query_ref in enumerate(queries):
        query = query_ref[...]
        chance = jax.nn.sigmoid(scale * dot(items, query, NT) + offset)
        if part == 0:
            own = lax.broadcasted_iota(I32, (examples, examples), 0) == lax.broadcasted_iota(
                I32, (examples, examples), 1
            )
            chance = chance - jnp.where(own, 1.0, 0.0)
        grad = grad + dot((chance * grad_scale).astype(BF16), query)
    slots = slot_matrix(listed_ref[...], capacity)
    sent_ref[...] = dot(slots, (grad * share).astype(BF16)).astype(BF16)


def update_kernel(
    wanted_ref, incoming_ref, table_ref, energy_ref, table_out_ref, energy_out_ref,
    row_ref, table_buf, energy_buf, sent, *, chunk, depth, piece,
):
    devices, capacity = wanted_ref.shape
    slots, _ = incoming_ref.shape
    rows = table_ref.shape[0]
    for s in range(devices):
        row_ref[:, s * capacity : (s + 1) * capacity] = jnp.broadcast_to(
            wanted_ref[s : s + 1, :], (8, capacity)
        )

    def stores(at):
        return (
            pltpu.make_async_copy(table_buf.at[at, :], table_out_ref.at[at, :], sent.at[0]),
            pltpu.make_async_copy(energy_buf.at[at, :], energy_out_ref.at[at, :], sent.at[1]),
        )

    def row_grad(base):
        here = lax.broadcasted_iota(I32, (chunk, 128), 0) + base
        total = None
        for k in range(0, slots, depth):
            hot = jnp.concatenate(
                [
                    one_hot(jnp.broadcast_to(row_ref[0:1, c : c + 128], (chunk, 128)) == here)
                    for c in range(k, k + depth, 128)
                ],
                axis=1,
            )
            part = dot(hot, incoming_ref[k : k + depth, :])
            total = part if total is None else total + part
        return total

    def adagrad(base, grad):
        at = pl.ds(pl.multiple_of(base, chunk), chunk)
        energy = energy_ref[at, :] + grad * grad
        energy_buf[at, :] = energy
        table_buf[at, :] = table_ref[at, :] - LEARN_RATE * grad / (jnp.sqrt(energy) + ADAGRAD_EPSILON)

    def sweep(i, carry):
        first = i * rows
        grad = row_grad(first)
        for q in range(chunk, rows + chunk, chunk):
            after = row_grad(first + q) if q < rows else None
            adagrad(first + q - chunk, grad)
            grad = after
            if q % piece == 0:
                for store in stores(pl.ds(pl.multiple_of(first + q - piece, piece), piece)):
                    store.start()
        return carry

    lax.fori_loop(0, 1, sweep, 0)
    for store in stores(pl.ds(0, rows)):
        store.wait()


def per_device(
    query_vectors,
    holding_devices,
    local_slot_number,
    valid_item_tally,
    score_stretch,
    offset_term,
    item_embedding_matrix,
    running_grad_energy,
):
    axes = ("shard", "blk")
    examples, bag = holding_devices.shape
    table_rows, width = item_embedding_matrix.shape
    devices = lax.axis_size(axes)
    blocks = lax.axis_size("blk")
    capacity = max(2, 2 * examples * bag // devices)
    slots = devices * capacity
    exchange = functools.partial(
        lax.all_to_all, axis_name=axes, split_axis=0, concat_axis=0, tiled=True
    )
    smem = pl.BlockSpec(memory_space=pltpu.SMEM)
    vmem = pl.BlockSpec(memory_space=pltpu.VMEM)
    hbm = pl.BlockSpec(memory_space=pltpu.HBM)

    def in_hbm(array):
        return pltpu.with_memory_space_constraint(array, pltpu.HBM)

    def limit(mib):
        return pltpu.CompilerParams(vmem_limit_bytes=mib * 1024 * 1024)

    def cost(gflops):
        return pl.CostEstimate(flops=gflops * 10**9, transcendentals=0, bytes_accessed=10**6)

    tally = valid_item_tally.reshape(1, examples)

    requests, listed = pl.pallas_call(
        route_kernel,
        out_shape=(
            jax.ShapeDtypeStruct((devices, capacity), I32),
            jax.ShapeDtypeStruct((devices, examples), I32),
        ),
        compiler_params=limit(4),
        cost_estimate=cost(10),
        name="route",
    )(in_hbm(holding_devices.T), in_hbm(local_slot_number.T), in_hbm(tally))
    wanted = exchange(requests)

    queries = [query_vectors]
    for step in range(1, blocks):
        queries.append(
            lax.ppermute(query_vectors, "blk", [(b, (b + step) % blocks) for b in range(blocks)])
        )
    out, share = pl.pallas_call(
        functools.partial(prepare_kernel, capacity=capacity),
        out_shape=(
            jax.ShapeDtypeStruct((examples, slots), BF16),
            jax.ShapeDtypeStruct((examples, 128), F32),
        ),
        compiler_params=limit(8),
        name="prepare",
    )(listed, in_hbm(tally))

    fetched = pl.pallas_call(
        functools.partial(fetch_kernel, step_rows=256, block=1024),
        in_specs=[vmem, vmem],
        out_shape=jax.ShapeDtypeStruct((slots, width), BF16),
        scratch_shapes=[pltpu.VMEM((slots, 128), I32)],
        compiler_params=limit(12),
        name="fetch",
    )(wanted, item_embedding_matrix)
    answered = exchange(fetched.reshape(devices, capacity, width)).reshape(slots, width)

    sent = pl.pallas_call(
        functools.partial(loss_kernel, capacity=capacity),
        in_specs=[smem, smem] + [vmem] * (4 + blocks),
        out_shape=jax.ShapeDtypeStruct((slots, width), BF16),
        compiler_params=limit(12),
        cost_estimate=cost(30),
        name="loss",
    )(score_stretch, offset_term, answered, listed, out, share, *queries)
    incoming = exchange(sent.reshape(devices, capacity, width)).reshape(slots, width)

    return pl.pallas_call(
        functools.partial(update_kernel, chunk=256, depth=1024, piece=256),
        in_specs=[vmem] * 4,
        out_specs=(hbm, hbm),
        out_shape=(
            jax.ShapeDtypeStruct((table_rows, width), F32),
            jax.ShapeDtypeStruct((table_rows, width), F32),
        ),
        scratch_shapes=[
            pltpu.VMEM((8, slots), I32),
            pltpu.VMEM((table_rows, width), F32),
            pltpu.VMEM((table_rows, width), F32),
            pltpu.SemaphoreType.DMA((2,)),
        ],
        compiler_params=limit(24),
        name="update",
    )(wanted, incoming, item_embedding_matrix, running_grad_energy)


def solution(mesh):
    rows = P(("shard", "blk"), None)
    placed = (rows, rows, rows, P(("shard", "blk")), P(), P(), rows, rows)
    return jax.shard_map(
        per_device, mesh=mesh, in_specs=placed, out_specs=(rows, rows), check_vma=False
    )
```
